32 devices in a mesh: shot: 4 (over x, core), band: 4 (over z), net: 2 (over y).
Axes of the slice: x: 2, y: 2, z: 4, core: 2. Of those that a mesh axis runs over, the one named last changes fastest.
Arguments:
- velocity: float32 [128, 1024], P('band'), may hold values from 1.5 to 4
- wave_now: float32 [16, 128, 1024], P(('shot', 'net'), 'band'), may hold values from -6 to 6
- wave_before: float32 [16, 128, 1024], P(('shot', 'net'), 'band'), may hold values from -6 to 6
- adjoint_last: float32 [16, 128, 1024], P(('shot', 'net'), 'band'), may hold values from -6 to 6
- adjoint_after: float32 [16, 128, 1024], P(('shot', 'net'), 'band'), may hold values from -6 to 6
- wavelet: float32 [16, 16], P(('shot', 'net')), may hold values from -72 to 72
- source_col: int32 [16], P(('shot', 'net')), may hold values from 0 to 1023
- rec_first: int32 [16], P(('shot', 'net')), may hold values from 0 to 1022
- rec_last: int32 [16], P(('shot', 'net')), may hold values from 1 to 1023
- rec_count: int32 [16], P(('shot', 'net')), may hold values from 2 to 128, as said below
- observed: float32 [16, 16, 128], P(('shot', 'net')), may hold values from -72 to 72
- conv_in: float32 [32, 18], replicated, may hold values from -1.5 to 1.5
- conv_mid: float32 [32, 288], replicated, may hold values from -0.375 to 0.375
- conv_out: float32 [1, 288], replicated, may hold values from -0.375 to 0.375
- cotangent: float32 [128, 1024], P('band', ('shot', 'net')), may hold values from -0.06629126 to 0.06629126
Outputs:
- new_velocity: float32 [128, 1024], P('band', ('shot', 'net'))
- grad_in: float32 [32, 18], replicated
- grad_mid: float32 [32, 288], replicated
- grad_out: float32 [1, 288], replicated
The draws below stay inside these ranges and needn't reach their ends.
Inputs may be any that keep to these rules, and one draw needn't show every extreme that they name: rec_last - rec_first >= rec_count - 1 for every shot; some shot has 128 receivers.
All inputs are finite; a program needn't handle non-finite values.
Results may differ from the reference program's by a relative error of at most 0.0003.
Values sent between devices are 32-bit elements; how exact they have to be, the bound alone decides.
A program may use at most 128 MiB of HBM per device.

```python
import math
import jax
import jax.numpy as jnp
from jax import lax

NT = 16
CH = 32
MAXREC = 128
NX = 128
NZ = 1024
SHOTS = 16


def receiver_draw(key):
    keys = jax.random.split(jax.random.fold_in(key, 7), 4)
    shot_ids = jnp.arange(SHOTS)
    chosen = jax.random.randint(keys[3], (), 0, SHOTS)
    fullest = shot_ids == chosen
    rightmost = shot_ids == (chosen + 1) % SHOTS
    leftmost = shot_ids == (chosen + 2) % SHOTS
    narrow = rightmost | leftmost
    counted = jax.random.randint(keys[0], (SHOTS,), 2, MAXREC + 1)
    counted = jnp.where(fullest, MAXREC, jnp.where(narrow, 2, counted))
    extra = jax.random.randint(keys[1], (SHOTS,), 0, NZ - counted + 1)
    span = jnp.where(narrow, 1, counted - 1 + extra)
    starts = jax.random.randint(keys[2], (SHOTS,), 0, NZ - span)
    starts = jnp.where(rightmost, NZ - 2, jnp.where(leftmost, 0, starts))
    return (starts.astype(jnp.int32), (starts + span).astype(jnp.int32), counted.astype(jnp.int32))


def draw_rec_first(key, part):
    return receiver_draw(key)[0]


def draw_rec_last(key, part):
    return receiver_draw(key)[1]


def draw_rec_count(key, part):
    return receiver_draw(key)[2]


def with_ends(values, rng, low, high):
    spot = [jax.random.randint(jax.random.fold_in(rng, axis), (), 0, length) for axis, length in enumerate(values.shape)]
    main_axis = values.shape.index(max(values.shape))
    next_to = spot[:main_axis] + [(spot[main_axis] + 1) % values.shape[main_axis]] + spot[main_axis + 1:]
    return values.at[tuple(spot)].set(low).at[tuple(next_to)].set(high)


def block_levels(own_key, extent, cuts, low, largest):
    def one(position, parts):
        draws = jax.random.uniform(jax.random.fold_in(jax.random.fold_in(own_key, 6), position), (parts,), jnp.float32, low / len(cuts), largest / len(cuts))
        return jnp.repeat(jnp.exp(draws), extent[position] // parts).reshape((-1,) + (1,) * (len(extent) - position - 1))

    factor_of = one(*cuts[0])
    for cut in cuts[1:]:
        factor_of = factor_of * one(*cut)
    return factor_of


def noise(key, shape, spread, bound, pieces=(), held_as=jnp.bfloat16):
    gain = block_levels(key, shape, pieces, -0.22, 0.18) if pieces else 1.0
    array = jax.random.normal(key, shape, jnp.float32) * spread * gain
    return jnp.minimum(jnp.maximum(array, -bound), bound).astype(held_as)


def setup_inputs(seed: int = 0) -> dict:
    key_list = jax.random.split(jax.random.key(seed), 16)
    velocity = jnp.clip(jnp.exp(math.log(4.0) - 0.98082925 * jax.random.uniform(key_list[0], (NX, NZ), jnp.float32) ** block_levels(key_list[0], (NX, NZ), ((0, 4),), -0.2, 0.2)), 1.5, 4.0)
    wave_now = noise(key_list[1], (SHOTS, NX, NZ), 1.0, 6.0, ((0, 8), (1, 4)), jnp.float32)
    wave_before = noise(key_list[2], (SHOTS, NX, NZ), 1.0, 6.0, ((0, 8), (1, 4)), jnp.float32)
    adjoint_last = noise(key_list[3], (SHOTS, NX, NZ), 1.0, 6.0, ((0, 8), (1, 4)), jnp.float32)
    adjoint_after = noise(key_list[4], (SHOTS, NX, NZ), 1.0, 6.0, ((0, 8), (1, 4)), jnp.float32)
    wavelet = noise(key_list[5], (SHOTS, NT), 12.0, 72.0, ((0, 8),), jnp.float32)
    source_col = with_ends(jax.random.randint(key_list[6], (SHOTS,), 0, NZ), jax.random.fold_in(key_list[6], 1), 0, NZ - 1).astype(jnp.int32)
    rec_first = draw_rec_first(jax.random.fold_in(key_list[15], 71), 0)
    rec_last = draw_rec_last(jax.random.fold_in(key_list[15], 71), 0)
    rec_count = draw_rec_count(jax.random.fold_in(key_list[15], 71), 0)
    observed = noise(key_list[10], (SHOTS, NT, MAXREC), 12.0, 72.0, ((0, 8),), jnp.float32)
    conv_in = noise(key_list[11], (CH, 18), 18 ** -0.5, 1.5, (), jnp.float32)
    conv_mid = noise(key_list[12], (CH, 9 * CH), (9 * CH) ** -0.5, 0.375, (), jnp.float32)
    conv_out = noise(key_list[13], (1, 9 * CH), (9 * CH) ** -0.5, 0.375, (), jnp.float32)
    cotangent = noise(key_list[14], (NX, NZ), (4.0 / (NX * NZ) ** 0.5), 0.06629126, ((0, 4), (1, 8)), jnp.float32)
    return {"velocity": velocity, "wave_now": wave_now, "wave_before": wave_before, "adjoint_last": adjoint_last, "adjoint_after": adjoint_after, "wavelet": wavelet, "source_col": source_col, "rec_first": rec_first, "rec_last": rec_last, "rec_count": rec_count, "observed": observed, "conv_in": conv_in, "conv_mid": conv_mid, "conv_out": conv_out, "cotangent": cotangent}


coefficients = (-205.0 / 72.0, 8.0 / 5.0, -1.0 / 5.0, 8.0 / 315.0, -1.0 / 560.0)
speed_factor = 0.11
source_depth = 2
receiver_depth = 3
highest = lax.Precision.HIGHEST

def laplace(extended):
    middle = extended[..., 4:-4, :]
    height = middle.shape[-2]
    breadth = middle.shape[-1]
    padding = [(0, 0)] * (middle.ndim - 1) + [(4, 4)]
    padded = jnp.pad(middle, padding)
    running = 2.0 * coefficients[0] * middle
    for reach in range(1, 5):
        vertical = extended[..., 4 - reach:4 - reach + height, :] + extended[..., 4 + reach:4 + reach + height, :]
        lateral = padded[..., 4 - reach:4 - reach + breadth] + padded[..., 4 + reach:4 + reach + breadth]
        running = running + coefficients[reach] * (vertical + lateral)
    return running

def receiver_table(rec_first, rec_last, rec_count, breadth, slots):
    columns = jnp.arange(breadth, dtype=jnp.int32)
    slot_ids = jnp.arange(slots, dtype=jnp.int32)
    placed = rec_first[:, None] + slot_ids[None, :] * (rec_last - rec_first)[:, None] // (rec_count - 1)[:, None]
    active = slot_ids[None, :] < rec_count[:, None]
    return ((columns[None, :, None] == placed[:, None, :]) & active[:, None, :]).astype(jnp.float32)

def convolve(field, weights):
    outputs = weights.shape[0]
    channels = field.shape[0]
    kernel = weights.reshape(outputs, 3, 3, channels).transpose(0, 3, 1, 2)
    return lax.conv_general_dilated(field[None], kernel, (1, 1), ((1, 1), (1, 1)), precision=highest)[0]

def network(first_weights, middle_weights, last_weights, velocity, scaled):
    layer_zero = jnp.stack([velocity, scaled])
    hidden_one = jax.nn.silu(convolve(layer_zero, first_weights))
    hidden_two = jax.nn.silu(convolve(hidden_one, middle_weights))
    return velocity + convolve(hidden_two, last_weights)[0]

def reference(velocity, wave_now, wave_before, adjoint_last, adjoint_after, wavelet, source_col, rec_first, rec_last, rec_count, observed, conv_in, conv_mid, conv_out, cotangent):
    speed_sq = (velocity * speed_factor) ** 2
    rows_all = jnp.arange(NX, dtype=jnp.int32)
    columns = jnp.arange(NZ, dtype=jnp.int32)
    source_rows = (rows_all == source_depth).astype(jnp.float32)[:, None]
    receiver_rows = (rows_all == receiver_depth).astype(jnp.float32)[:, None]
    tables = receiver_table(rec_first, rec_last, rec_count, NZ, MAXREC)
    active = (jnp.arange(MAXREC, dtype=jnp.int32)[None, :] < rec_count[:, None]).astype(jnp.float32)

    def advance(current, earlier, term):
        extended = jnp.pad(current, ((4, 4), (0, 0)))
        return 2.0 * current - earlier + speed_sq * laplace(extended) + term

    def one_shot(running, shot):
        start, prior, adjoint_start, adjoint_prior, pulses, place, table, recorded, live = shot
        source_field = source_rows * (columns == place).astype(jnp.float32)[None, :]

        def forward(carry, amount):
            fresh = advance(carry[0], carry[1], amount * source_field)
            return ((fresh, carry[0]), fresh)
        ignored, stored = lax.scan(forward, (start, prior), pulses)
        samples = jnp.dot(stored[:, receiver_depth, :], table, precision=highest)
        misfit = (samples - recorded) * live[None, :]

        def backward(carry, inputs):
            field, residual = inputs
            injected = receiver_rows * jnp.dot(table, residual, precision=highest)[None, :]
            fresh = advance(carry[0], carry[1], injected)
            return ((fresh, carry[0], carry[2] + field * fresh), None)
        final, unused = lax.scan(backward, (adjoint_start, adjoint_prior, running), (stored, misfit), reverse=True)
        return (final[2], None)
    image, ignored = lax.scan(one_shot, jnp.zeros((NX, NZ), jnp.float32), (wave_now, wave_before, adjoint_last, adjoint_after, wavelet, source_col, tables, observed, active))
    scaled = image / float(NT * SHOTS) ** 0.5

    def apply(first_weights, middle_weights, last_weights):
        return network(first_weights, middle_weights, last_weights, velocity, scaled)
    new_velocity, pullback = jax.vjp(apply, conv_in, conv_mid, conv_out)
    grads = pullback(cotangent)
    return (new_velocity, grads[0], grads[1], grads[2])
```

```python
import functools

import jax
import jax.numpy as jnp
import numpy as np
from jax import lax
from jax.experimental import pallas as pl
from jax.experimental.pallas import tpu as pltpu
from jax.sharding import PartitionSpec as P

coefficients = (-205.0 / 72.0, 8.0 / 5.0, -1.0 / 5.0, 8.0 / 315.0, -1.0 / 560.0)
speed_factor = 0.11
source_depth = 2
receiver_depth = 3
highest = lax.Precision.HIGHEST


def extended_2(block, sides, width):
    for axis, dim in sides:
        count = lax.axis_size(axis)
        forward = [(i, i + 1) for i in range(count - 1)]
        backward = [(target, source) for source, target in forward]
        low = lax.ppermute(
            lax.slice_in_dim(block, block.shape[dim] - width, None, axis=dim), axis, forward
        )
        high = lax.ppermute(lax.slice_in_dim(block, 0, width, axis=dim), axis, backward)
        block = jnp.concatenate([low, block, high], axis=dim)
    return block


def laplace(extended):
    middle = extended[..., 4:-4, :]
    height = middle.shape[-2]
    breadth = middle.shape[-1]
    padding = [(0, 0)] * (middle.ndim - 1) + [(4, 4)]
    padded = jnp.pad(middle, padding)
    running = 2.0 * coefficients[0] * middle
    for reach in range(1, 5):
        vertical = (
            extended[..., 4 - reach : 4 - reach + height, :]
            + extended[..., 4 + reach : 4 + reach + height, :]
        )
        lateral = (
            padded[..., 4 - reach : 4 - reach + breadth]
            + padded[..., 4 + reach : 4 + reach + breadth]
        )
        running = running + coefficients[reach] * (vertical + lateral)
    return running


def receiver_table(rec_first, rec_last, rec_count, breadth, slots):
    columns = jnp.arange(breadth, dtype=jnp.int32)
    slot_ids = jnp.arange(slots, dtype=jnp.int32)
    placed = (
        rec_first[:, None]
        + slot_ids[None, :] * (rec_last - rec_first)[:, None] // (rec_count - 1)[:, None]
    )
    active = slot_ids[None, :] < rec_count[:, None]
    return ((columns[None, :, None] == placed[:, None, :]) & active[:, None, :]).astype(jnp.float32)


def flipped(weights):
    outputs = weights.shape[0]
    channels = weights.shape[1] // 9
    return (
        weights.reshape(outputs, 9, channels)[:, ::-1, :]
        .transpose(2, 1, 0)
        .reshape(channels, 9 * outputs)
    )


MESH = pl.DeviceIdType.MESH
group_axes = ("shot", "net")
chunk = 512


def vmem(count):
    return [pl.BlockSpec(memory_space=pltpu.VMEM)] * count


def remote(source, target, send, receive, device):
    return pltpu.make_async_remote_copy(
        src_ref=source,
        dst_ref=target,
        send_sem=send,
        recv_sem=receive,
        device_id=device,
        device_id_type=MESH,
    )


def gather_kernel(
    groups, nets, bands, image, velocity, cotangent,
    out_image, out_cot, out_low, out_high,
    padded, slots, total, halo, speed_halo,
    send, receive, side_send, side_receive, row_send, row_receive,
):
    rows, breadth = image.shape
    piece = cotangent.shape[1]
    shot = lax.axis_index("shot")
    net = lax.axis_index("net")
    band = lax.axis_index("band")
    me = shot * nets + net

    def member(index):
        return {"shot": index // nets, "net": lax.rem(index, nets)}

    total[1] = jnp.zeros((rows, 3 * piece), jnp.float32)
    halo[...] = jnp.zeros(halo.shape, jnp.float32)
    speed_halo[...] = jnp.zeros(speed_halo.shape, jnp.float32)
    barrier = pltpu.get_barrier_semaphore()
    for step in range(1, groups):
        pl.semaphore_signal(
            barrier, inc=1, device_id=member(lax.rem(me + step, groups)), device_id_type=MESH
        )

    @pl.when(band > 0)
    def _():
        pl.semaphore_signal(barrier, inc=1, device_id={"band": band - 1}, device_id_type=MESH)

    @pl.when(band < bands - 1)
    def _():
        pl.semaphore_signal(barrier, inc=1, device_id={"band": band + 1}, device_id_type=MESH)

    padded[:, :piece] = jnp.zeros((rows, piece), jnp.float32)
    padded[:, piece + breadth :] = jnp.zeros((rows, piece), jnp.float32)
    padded[:, piece : piece + breadth] = image[...]
    pl.semaphore_wait(
        barrier, groups - 1 + lax.min(band, 1) + lax.min(bands - 1 - band, 1)
    )

    def scatter(step):
        target = lax.rem(me + step, groups)
        start = pl.multiple_of(target * piece, 128)
        return remote(
            padded.at[:, pl.ds(start, 3 * piece)],
            slots.at[step],
            send.at[step],
            receive.at[step],
            member(target),
        )

    for step in range(1, groups):
        scatter(step).start()

    def to_right():
        return remote(
            cotangent, total.at[1, :, pl.ds(0, piece)], side_send.at[0], side_receive.at[0],
            member(me + 1),
        )

    def to_left():
        return remote(
            cotangent, total.at[1, :, pl.ds(2 * piece, piece)], side_send.at[1],
            side_receive.at[1], member(me - 1),
        )

    def speed_up():
        return remote(
            velocity.at[pl.ds(0, 8)], speed_halo.at[1], row_send.at[0], row_receive.at[0],
            {"band": band - 1},
        )

    def speed_down():
        return remote(
            velocity.at[pl.ds(rows - 8, 8)], speed_halo.at[0], row_send.at[1], row_receive.at[1],
            {"band": band + 1},
        )

    def field_up():
        return remote(
            total.at[:, pl.ds(0, 8)], halo.at[1], row_send.at[2], row_receive.at[2],
            {"band": band - 1},
        )

    def field_down():
        return remote(
            total.at[:, pl.ds(rows - 8, 8)], halo.at[0], row_send.at[3], row_receive.at[3],
            {"band": band + 1},
        )

    pl.when(me < groups - 1)(lambda: to_right().start())
    pl.when(me > 0)(lambda: to_left().start())
    pl.when(band > 0)(lambda: speed_up().start())
    pl.when(band < bands - 1)(lambda: speed_down().start())

    own = pl.multiple_of(me * piece, 128)
    slots[0] = padded[:, pl.ds(own, 3 * piece)]
    for step in range(1, groups):
        scatter(step).wait_recv()
    summed = slots[0]
    for step in range(1, groups):
        summed = summed + slots[step]
    total[0] = summed
    pl.when(me > 0)(lambda: to_right().wait_recv())
    pl.when(me < groups - 1)(lambda: to_left().wait_recv())
    total[1, :, piece : 2 * piece] = cotangent[...]
    pl.when(band > 0)(lambda: field_up().start())
    pl.when(band < bands - 1)(lambda: field_down().start())
    for step in range(1, groups):
        scatter(step).wait_send()
    pl.when(me < groups - 1)(lambda: to_right().wait_send())
    pl.when(me > 0)(lambda: to_left().wait_send())
    pl.when(band > 0)(lambda: speed_up().wait_send())
    pl.when(band < bands - 1)(lambda: speed_down().wait_send())
    pl.when(band > 0)(lambda: speed_down().wait_recv())
    pl.when(band < bands - 1)(lambda: speed_up().wait_recv())
    pl.when(band > 0)(lambda: field_up().wait_send())
    pl.when(band < bands - 1)(lambda: field_down().wait_send())
    pl.when(band > 0)(lambda: field_down().wait_recv())
    pl.when(band < bands - 1)(lambda: field_up().wait_recv())
    for which, target in ((0, out_image), (1, out_cot)):
        target[0:8] = halo[0, which]
        target[8 : 8 + rows] = total[which]
        target[8 + rows :] = halo[1, which]
    out_low[...] = speed_halo[0]
    out_high[...] = speed_halo[1]


def gather_pieces(image, velocity, cotangent):
    rows, breadth = image.shape
    piece = cotangent.shape[1]
    groups = lax.axis_size(group_axes)
    nets = lax.axis_size("net")
    bands = lax.axis_size("band")
    f32 = jnp.float32
    dma = pltpu.SemaphoreType.DMA
    return pl.pallas_call(
        functools.partial(gather_kernel, groups, nets, bands),
        name="gather_pieces",
        out_shape=[jax.ShapeDtypeStruct((rows + 16, 3 * piece), f32)] * 2
        + [jax.ShapeDtypeStruct((8, breadth), f32)] * 2,
        in_specs=vmem(3),
        out_specs=vmem(4),
        scratch_shapes=[
            pltpu.VMEM((rows, breadth + 2 * piece), f32),
            pltpu.VMEM((groups, rows, 3 * piece), f32),
            pltpu.VMEM((2, rows, 3 * piece), f32),
            pltpu.VMEM((2, 2, 8, 3 * piece), f32),
            pltpu.VMEM((2, 8, breadth), f32),
            dma((groups,)),
            dma((groups,)),
            dma((2,)),
            dma((2,)),
            dma((4,)),
            dma((4,)),
        ],
        compiler_params=pltpu.CompilerParams(collective_id=1, has_side_effects=True),
    )(image, velocity, cotangent)


def total_kernel(sizes, grads, out, shot_slots, net_slots, band_slots, ready, send, receive):
    part = grads.shape[0] // sizes["shot"]
    barrier = pltpu.get_barrier_semaphore()
    count = 0
    for axis, size in sizes.items():
        me = lax.axis_index(axis)
        for step in range(1, size):
            pl.semaphore_signal(
                barrier, inc=1, device_id={axis: lax.rem(me + step, size)}, device_id_type=MESH
            )
            count += 1
    pl.semaphore_wait(barrier, count)
    base = 0

    def stage(axis, source, target_of, base):
        size = sizes[axis]
        me = lax.axis_index(axis)

        def copy(step, sender):
            peer = lax.rem(me + step, size)
            return remote(
                source(peer), target_of(sender), send.at[base + step], receive.at[base + sender],
                {axis: peer},
            )

        for step in range(1, size):
            copy(step, me).start()
        return copy, size, me

    def finish(handle):
        copy, size, me = handle
        for step in range(1, size):
            copy(step, lax.rem(me + step, size)).wait_recv()
        for step in range(1, size):
            copy(step, me).wait_send()

    shot = lax.axis_index("shot")
    handle = stage(
        "shot",
        lambda peer: grads.at[pl.ds(pl.multiple_of(peer * part, 8), part)],
        lambda sender: shot_slots.at[sender],
        0,
    )
    shot_slots[shot] = grads[pl.ds(pl.multiple_of(shot * part, 8), part)]
    finish(handle)

    def add(slots):
        running = slots[0]
        for index in range(1, slots.shape[0]):
            running = running + slots[index]
        return running

    base = sizes["shot"]
    ready[0] = add(shot_slots)
    handle = stage("net", lambda peer: ready.at[0], lambda sender: net_slots.at[sender], base)
    net_slots[lax.axis_index("net")] = ready[0]
    finish(handle)
    base += sizes["net"]
    ready[1] = add(net_slots)
    handle = stage("band", lambda peer: ready.at[1], lambda sender: band_slots.at[sender], base)
    band_slots[lax.axis_index("band")] = ready[1]
    finish(handle)
    base += sizes["band"]
    ready[2] = add(band_slots)
    handle = stage(
        "shot",
        lambda peer: ready.at[2],
        lambda sender: out.at[pl.ds(pl.multiple_of(sender * part, 8), part)],
        base,
    )
    out[pl.ds(pl.multiple_of(shot * part, 8), part)] = ready[2]
    finish(handle)


def total_grads(grads):
    sizes = {axis: lax.axis_size(axis) for axis in ("shot", "net", "band")}
    part = (grads.shape[0] // sizes["shot"], grads.shape[1])
    f32 = jnp.float32
    count = 2 * sizes["shot"] + sizes["net"] + sizes["band"]
    return pl.pallas_call(
        functools.partial(total_kernel, sizes),
        name="total_grads",
        out_shape=jax.ShapeDtypeStruct(grads.shape, f32),
        in_specs=vmem(1),
        out_specs=vmem(1)[0],
        scratch_shapes=[
            pltpu.VMEM((sizes["shot"],) + part, f32),
            pltpu.VMEM((sizes["net"],) + part, f32),
            pltpu.VMEM((sizes["band"],) + part, f32),
            pltpu.VMEM((3,) + part, f32),
            pltpu.SemaphoreType.DMA((count,)),
            pltpu.SemaphoreType.DMA((count,)),
        ],
        compiler_params=pltpu.CompilerParams(collective_id=2, has_side_effects=True),
    )(grads)


def halves(values):
    high = values.astype(jnp.bfloat16)
    return high, (values - high.astype(jnp.float32)).astype(jnp.bfloat16)


def dot3(left, right_high, right_low, dims):
    high, low = halves(left)
    height = left.shape[0]
    both = lax.dot_general(
        jnp.concatenate([high, low], 0), right_high, (dims, ((), ())),
        preferred_element_type=jnp.float32,
    )
    rest = lax.dot_general(
        high, right_low, (dims, ((), ())), preferred_element_type=jnp.float32
    )
    return both[:height] + both[height:] + rest


def network_kernel(
    width, first, middle, middle_back, last, layers,
    new_velocity, grads,
    patch_zero, patch_high, patch_low, before_one, hidden, slope_two, last_taps,
):
    length = layers.shape[1]
    channels = middle.shape[0]
    shifts = [down * width + across for down in (-1, 0, 1) for across in (-1, 0, 1)]
    pieces = length // chunk
    flat = ((1,), (0,))
    over = ((1,), (1,))

    for tap, shift in enumerate(shifts):
        patch_zero[tap * 8 : tap * 8 + 8] = pltpu.roll(layers[...], (-shift) % length, 1)

    def spread(source):
        for group in range(channels // 16):
            rows = source[group * 16 : group * 16 + 16]
            for tap, shift in enumerate(shifts):
                high, low = halves(pltpu.roll(rows, (-shift) % length, 1))
                start = tap * channels + group * 16
                patch_high[start : start + 16] = high
                patch_low[start : start + 16] = low

    def each(body, init=0):
        def step(index, carry):
            return body(pl.ds(pl.multiple_of(index * chunk, chunk), chunk), carry)

        return lax.fori_loop(0, pieces, step, init)

    def slope(values):
        squashed = 1.0 / (1.0 + jnp.exp(-values))
        return squashed * (1.0 + values * (1.0 - squashed))

    def silu(values):
        return values / (1.0 + jnp.exp(-values))

    def open_layer(at, carry):
        high, low = halves(patch_zero[:, at])
        both = dot3(first[...], high, low, flat)
        inside = layers[4:5, at] > 0.5
        before = both[:channels]
        before_one[:, at] = before
        hidden[:, at] = jnp.where(inside, silu(before), 0.0)
        slope_two[:, at] = both[channels:]
        return carry

    each(open_layer)
    spread(hidden)

    def middle_layer(at, carry):
        high = patch_high[:, at]
        low = patch_low[:, at]
        before = dot3(middle[...], high, low, flat)
        inside = layers[4:5, at] > 0.5
        owned = layers[5:6, at] > 0.5
        after = jnp.where(inside, silu(before), 0.0)
        hidden[:, at] = after
        fall = jnp.where(inside, slope_two[:, at] * slope(before), 0.0)
        slope_two[:, at] = fall
        after_high, after_low = halves(after)
        last_taps[:, at] = dot3(last[...], after_high, after_low, flat)
        return carry + dot3(jnp.where(owned, fall, 0.0), high, low, over)

    grad_middle = each(middle_layer, jnp.zeros((channels, 9 * channels), jnp.float32))
    spread(slope_two)
    update = layers[0:1]
    for tap, shift in enumerate(shifts):
        update = update + pltpu.roll(last_taps[...], (-shift) % length, 1)[tap : tap + 1]
    new_velocity[...] = update

    def first_grads(at, carry):
        back = dot3(middle_back[...], patch_high[:, at], patch_low[:, at], flat)
        owned = layers[5:6, at] > 0.5
        fall = jnp.where(owned, back * slope(before_one[:, at]), 0.0)
        high, low = halves(patch_zero[:, at])
        return carry + dot3(jnp.concatenate([fall, hidden[:, at]], 0), high, low, over)

    outer = each(first_grads, jnp.zeros((2 * channels, 72), jnp.float32))
    grads[...] = jnp.zeros(grads.shape, jnp.float32)
    grads[:, 0 : 9 * channels] = grad_middle
    start = -(-9 * channels // 128) * 128
    grads[:, start : start + 72] = outer[:channels]
    grads[:, start + 128 : start + 200] = outer[channels:]


def network(layers, width, conv_in, conv_mid, conv_out):
    length = layers.shape[1]
    channels = conv_mid.shape[0]
    f32 = jnp.float32
    taken = conv_in.reshape(channels, 9, 2)
    first = jnp.concatenate(
        [
            jnp.pad(taken, ((0, 0), (0, 0), (0, 6))).reshape(channels, 72),
            jnp.pad(flipped(conv_out)[:, :, None], ((0, 0), (0, 0), (2, 5))).reshape(channels, 72),
        ],
        0,
    )
    last = jnp.pad(conv_out.reshape(9, channels), ((0, 7), (0, 0)))
    start = -(-9 * channels // 128) * 128
    return pl.pallas_call(
        functools.partial(network_kernel, width),
        name="network",
        out_shape=[
            jax.ShapeDtypeStruct((1, length), f32),
            jax.ShapeDtypeStruct((channels, start + 256), f32),
        ],
        in_specs=vmem(5),
        out_specs=vmem(2),
        scratch_shapes=[
            pltpu.VMEM((72, length), f32),
            pltpu.VMEM((9 * channels, length), jnp.bfloat16),
            pltpu.VMEM((9 * channels, length), jnp.bfloat16),
            pltpu.VMEM((channels, length), f32),
            pltpu.VMEM((channels, length), f32),
            pltpu.VMEM((channels, length), f32),
            pltpu.VMEM((16, length), f32),
        ],
        compiler_params=pltpu.CompilerParams(vmem_limit_bytes=48 * 1024 * 1024),
    )(first, conv_mid, flipped(conv_mid), last, layers)


def update_model(imaging, velocity, cotangent, num_steps, shot_count, conv_in, conv_mid, conv_out):
    rows, breadth = velocity.shape
    piece = cotangent.shape[1]
    channels = conv_mid.shape[0]
    bands = lax.axis_size("band")
    groups = lax.axis_size(group_axes)
    image, cot, low, high = gather_pieces(imaging, velocity, cotangent)
    scaled = image[5:-5, piece - 3 : 2 * piece + 3] / float(num_steps * shot_count) ** 0.5
    cot = cot[5:-5, piece - 3 : 2 * piece + 3]
    tall = jnp.concatenate([low[5:], velocity, high[:3]], 0)
    start_col = lax.axis_index(group_axes) * piece
    around = lax.dynamic_slice_in_dim(
        jnp.pad(tall, ((0, 0), (piece, piece))), start_col, 3 * piece, 1
    )[:, piece - 3 : 2 * piece + 3]
    height, width = around.shape
    row_ids = lax.axis_index("band") * rows - 3 + jnp.arange(height)
    col_ids = start_col - 3 + jnp.arange(width)
    inside = ((row_ids >= 0) & (row_ids < rows * bands))[:, None] & (
        (col_ids >= 0) & (col_ids < piece * groups)
    )[None, :]
    owned = np.zeros((height, width), np.float32)
    owned[3:-3, 3:-3] = 1.0
    blank = jnp.zeros((height, width), jnp.float32)
    layers = jnp.stack(
        [around, scaled, cot, cot * owned, inside.astype(jnp.float32), jnp.asarray(owned), blank, blank]
    ).reshape(8, height * width)
    length = -(-height * width // chunk) * chunk
    layers = jnp.pad(layers, ((0, 0), (0, length - height * width)))
    fresh, grads = network(layers, width, conv_in, conv_mid, conv_out)
    new_velocity = fresh[0, : height * width].reshape(height, width)[3:-3, 3:-3]
    grads = total_grads(grads)
    start = -(-9 * channels // 128) * 128
    grad_in = grads[:, start : start + 72].reshape(channels, 9, 8)[:, :, :2].reshape(channels, 18)
    spare = grads[:, start + 128 : start + 200].reshape(channels, 9, 8)[:, ::-1, 3]
    return new_velocity, grad_in, grads[:, : 9 * channels], spare.T.reshape(1, 9 * channels)


def on_device(
    velocity,
    wave_now,
    wave_before,
    adjoint_last,
    adjoint_after,
    wavelet,
    source_col,
    rec_first,
    rec_last,
    rec_count,
    observed,
    conv_in,
    conv_mid,
    conv_out,
    cotangent,
):
    rows_here = velocity.shape[0]
    breadth = velocity.shape[1]
    shot_here = wave_now.shape[0]
    num_steps = wavelet.shape[1]
    slots = observed.shape[2]
    piece_cols = cotangent.shape[1]
    first_row = lax.axis_index("band") * rows_here
    speed_sq = (velocity * speed_factor) ** 2
    columns = jnp.arange(breadth, dtype=jnp.int32)
    source_cols = (columns[None, :] == source_col[:, None]).astype(jnp.float32)[:, None, :]
    table = receiver_table(rec_first, rec_last, rec_count, breadth, slots)
    active = (jnp.arange(slots, dtype=jnp.int32)[None, :] < rec_count[:, None]).astype(jnp.float32)

    def source_term(row_start, height, amount):
        row_ids = row_start + jnp.arange(height, dtype=jnp.int32)
        marked = (row_ids == source_depth).astype(jnp.float32)[None, :, None]
        return marked * source_cols * amount[:, None, None]

    def receiver_term(row_start, height, residual):
        row_ids = row_start + jnp.arange(height, dtype=jnp.int32)
        marked = (row_ids == receiver_depth).astype(jnp.float32)[None, :, None]
        injected = jnp.einsum("swk,sk->sw", table, residual, precision=highest)
        return marked * injected[:, None, :]

    speed_wide = extended_2(speed_sq, (("band", 0),), 16)

    def propagate(start, prior, drive, inject):
        grouped = drive.reshape((num_steps // 4, 4) + drive.shape[1:])

        def block(carry, amounts):
            stacked = extended_2(jnp.stack([carry[0], carry[1]]), (("band", 2),), 16)
            current = stacked[0]
            earlier = stacked[1]
            margin = 16
            saved = []
            for offset in range(4):
                inner = margin - 4
                speed_part = speed_wide[16 - inner : 16 + rows_here + inner]
                fresh = (
                    2.0 * current[:, 4:-4]
                    - earlier[:, 4:-4]
                    + speed_part * laplace(current)
                    + inject(first_row - inner, rows_here + 2 * inner, amounts[offset])
                )
                earlier = current[:, 4:-4]
                current = fresh
                margin = inner
                saved.append(fresh[:, inner : inner + rows_here])
            return ((current, earlier), jnp.stack(saved))

        ignored, states = lax.scan(block, (start, prior), grouped)
        return states.reshape((num_steps,) + start.shape)

    stored = propagate(wave_now, wave_before, wavelet.T, source_term)
    samples = jnp.einsum("tsw,swk->tsk", stored[:, :, receiver_depth, :], table, precision=highest)
    misfit = (samples - jnp.transpose(observed, (1, 0, 2))) * active[None]
    adjoint = propagate(adjoint_last, adjoint_after, misfit[::-1], receiver_term)
    imaging = jnp.sum(stored * adjoint[::-1], axis=(0, 1))
    group_count = shot_here * lax.axis_size(("shot", "net"))
    return update_model(
        imaging, velocity, cotangent, num_steps, group_count, conv_in, conv_mid, conv_out
    )


def solution(mesh):
    in_specs = (
        P("band", None),
        P(("shot", "net"), "band", None),
        P(("shot", "net"), "band", None),
        P(("shot", "net"), "band", None),
        P(("shot", "net"), "band", None),
        P(("shot", "net"), None),
        P(("shot", "net")),
        P(("shot", "net")),
        P(("shot", "net")),
        P(("shot", "net")),
        P(("shot", "net"), None, None),
        P(),
        P(),
        P(),
        P("band", ("shot", "net")),
    )
    out_specs = (P("band", ("shot", "net")), P(), P(), P())
    return jax.shard_map(
        on_device, mesh=mesh, in_specs=in_specs, out_specs=out_specs, check_vma=False
    )
```

```python
import functools

import jax
import jax.numpy as jnp
import numpy as np
from jax import lax
from jax.experimental import pallas as pl
from jax.experimental.pallas import tpu as pltpu
from jax.sharding import PartitionSpec as P

coefficients = (-205.0 / 72.0, 8.0 / 5.0, -1.0 / 5.0, 8.0 / 315.0, -1.0 / 560.0)
speed_factor = 0.11
source_depth = 2
receiver_depth = 3
highest = lax.Precision.HIGHEST


def receiver_table(rec_first, rec_last, rec_count, breadth, slots):
    columns = jnp.arange(breadth, dtype=jnp.int32)
    slot_ids = jnp.arange(slots, dtype=jnp.int32)
    placed = (
        rec_first[:, None]
        + slot_ids[None, :] * (rec_last - rec_first)[:, None] // (rec_count - 1)[:, None]
    )
    active = slot_ids[None, :] < rec_count[:, None]
    return ((columns[None, :, None] == placed[:, None, :]) & active[:, None, :]).astype(jnp.float32)


def flipped(weights):
    outputs = weights.shape[0]
    channels = weights.shape[1] // 9
    return (
        weights.reshape(outputs, 9, channels)[:, ::-1, :]
        .transpose(2, 1, 0)
        .reshape(channels, 9 * outputs)
    )


MESH = pl.DeviceIdType.MESH
group_axes = ("shot", "net")
chunk = 512


def vmem(count):
    return [pl.BlockSpec(memory_space=pltpu.VMEM)] * count


def remote(source, target, send, receive, device):
    return pltpu.make_async_remote_copy(
        src_ref=source,
        dst_ref=target,
        send_sem=send,
        recv_sem=receive,
        device_id=device,
        device_id_type=MESH,
    )


def gather_kernel(
    groups, nets, bands, image, velocity, cotangent,
    out_image, out_cot, out_low, out_high,
    padded, slots, total, halo, speed_halo,
    send, receive, side_send, side_receive, row_send, row_receive,
):
    rows, breadth = image.shape
    piece = cotangent.shape[1]
    shot = lax.axis_index("shot")
    net = lax.axis_index("net")
    band = lax.axis_index("band")
    me = shot * nets + net

    def member(index):
        return {"shot": index // nets, "net": lax.rem(index, nets)}

    total[1] = jnp.zeros((rows, 3 * piece), jnp.float32)
    halo[...] = jnp.zeros(halo.shape, jnp.float32)
    speed_halo[...] = jnp.zeros(speed_halo.shape, jnp.float32)
    barrier = pltpu.get_barrier_semaphore()
    for step in range(1, groups):
        pl.semaphore_signal(
            barrier, inc=1, device_id=member(lax.rem(me + step, groups)), device_id_type=MESH
        )

    @pl.when(band > 0)
    def _():
        pl.semaphore_signal(barrier, inc=1, device_id={"band": band - 1}, device_id_type=MESH)

    @pl.when(band < bands - 1)
    def _():
        pl.semaphore_signal(barrier, inc=1, device_id={"band": band + 1}, device_id_type=MESH)

    padded[:, :piece] = jnp.zeros((rows, piece), jnp.float32)
    padded[:, piece + breadth :] = jnp.zeros((rows, piece), jnp.float32)
    padded[:, piece : piece + breadth] = image[...]
    pl.semaphore_wait(
        barrier, groups - 1 + lax.min(band, 1) + lax.min(bands - 1 - band, 1)
    )

    def scatter(step):
        target = lax.rem(me + step, groups)
        start = pl.multiple_of(target * piece, 128)
        return remote(
            padded.at[:, pl.ds(start, 3 * piece)],
            slots.at[step],
            send.at[step],
            receive.at[step],
            member(target),
        )

    for step in range(1, groups):
        scatter(step).start()

    def to_right():
        return remote(
            cotangent, total.at[1, :, pl.ds(0, piece)], side_send.at[0], side_receive.at[0],
            member(me + 1),
        )

    def to_left():
        return remote(
            cotangent, total.at[1, :, pl.ds(2 * piece, piece)], side_send.at[1],
            side_receive.at[1], member(me - 1),
        )

    def speed_up():
        return remote(
            velocity.at[pl.ds(0, 8)], speed_halo.at[1], row_send.at[0], row_receive.at[0],
            {"band": band - 1},
        )

    def speed_down():
        return remote(
            velocity.at[pl.ds(rows - 8, 8)], speed_halo.at[0], row_send.at[1], row_receive.at[1],
            {"band": band + 1},
        )

    def field_up():
        return remote(
            total.at[:, pl.ds(0, 8)], halo.at[1], row_send.at[2], row_receive.at[2],
            {"band": band - 1},
        )

    def field_down():
        return remote(
            total.at[:, pl.ds(rows - 8, 8)], halo.at[0], row_send.at[3], row_receive.at[3],
            {"band": band + 1},
        )

    pl.when(me < groups - 1)(lambda: to_right().start())
    pl.when(me > 0)(lambda: to_left().start())
    pl.when(band > 0)(lambda: speed_up().start())
    pl.when(band < bands - 1)(lambda: speed_down().start())

    own = pl.multiple_of(me * piece, 128)
    slots[0] = padded[:, pl.ds(own, 3 * piece)]
    for step in range(1, groups):
        scatter(step).wait_recv()
    summed = slots[0]
    for step in range(1, groups):
        summed = summed + slots[step]
    total[0] = summed
    pl.when(me > 0)(lambda: to_right().wait_recv())
    pl.when(me < groups - 1)(lambda: to_left().wait_recv())
    total[1, :, piece : 2 * piece] = cotangent[...]
    pl.when(band > 0)(lambda: field_up().start())
    pl.when(band < bands - 1)(lambda: field_down().start())
    for step in range(1, groups):
        scatter(step).wait_send()
    pl.when(me < groups - 1)(lambda: to_right().wait_send())
    pl.when(me > 0)(lambda: to_left().wait_send())
    pl.when(band > 0)(lambda: speed_up().wait_send())
    pl.when(band < bands - 1)(lambda: speed_down().wait_send())
    pl.when(band > 0)(lambda: speed_down().wait_recv())
    pl.when(band < bands - 1)(lambda: speed_up().wait_recv())
    pl.when(band > 0)(lambda: field_up().wait_send())
    pl.when(band < bands - 1)(lambda: field_down().wait_send())
    pl.when(band > 0)(lambda: field_down().wait_recv())
    pl.when(band < bands - 1)(lambda: field_up().wait_recv())
    for which, target in ((0, out_image), (1, out_cot)):
        target[0:8] = halo[0, which]
        target[8 : 8 + rows] = total[which]
        target[8 + rows :] = halo[1, which]
    out_low[...] = speed_halo[0]
    out_high[...] = speed_halo[1]


def gather_pieces(image, velocity, cotangent):
    rows, breadth = image.shape
    piece = cotangent.shape[1]
    groups = lax.axis_size(group_axes)
    nets = lax.axis_size("net")
    bands = lax.axis_size("band")
    f32 = jnp.float32
    dma = pltpu.SemaphoreType.DMA
    return pl.pallas_call(
        functools.partial(gather_kernel, groups, nets, bands),
        name="gather_pieces",
        out_shape=[jax.ShapeDtypeStruct((rows + 16, 3 * piece), f32)] * 2
        + [jax.ShapeDtypeStruct((8, breadth), f32)] * 2,
        in_specs=vmem(3),
        out_specs=vmem(4),
        scratch_shapes=[
            pltpu.VMEM((rows, breadth + 2 * piece), f32),
            pltpu.VMEM((groups, rows, 3 * piece), f32),
            pltpu.VMEM((2, rows, 3 * piece), f32),
            pltpu.VMEM((2, 2, 8, 3 * piece), f32),
            pltpu.VMEM((2, 8, breadth), f32),
            dma((groups,)),
            dma((groups,)),
            dma((2,)),
            dma((2,)),
            dma((4,)),
            dma((4,)),
        ],
        compiler_params=pltpu.CompilerParams(collective_id=1, has_side_effects=True),
    )(image, velocity, cotangent)


def total_kernel(sizes, grads, out, shot_slots, net_slots, band_slots, ready, send, receive):
    part = grads.shape[0] // sizes["shot"]
    barrier = pltpu.get_barrier_semaphore()
    count = 0
    for axis, size in sizes.items():
        me = lax.axis_index(axis)
        for step in range(1, size):
            pl.semaphore_signal(
                barrier, inc=1, device_id={axis: lax.rem(me + step, size)}, device_id_type=MESH
            )
            count += 1
    pl.semaphore_wait(barrier, count)
    base = 0

    def stage(axis, source, target_of, base):
        size = sizes[axis]
        me = lax.axis_index(axis)

        def copy(step, sender):
            peer = lax.rem(me + step, size)
            return remote(
                source(peer), target_of(sender), send.at[base + step], receive.at[base + sender],
                {axis: peer},
            )

        for step in range(1, size):
            copy(step, me).start()
        return copy, size, me

    def finish(handle):
        copy, size, me = handle
        for step in range(1, size):
            copy(step, lax.rem(me + step, size)).wait_recv()
        for step in range(1, size):
            copy(step, me).wait_send()

    shot = lax.axis_index("shot")
    handle = stage(
        "shot",
        lambda peer: grads.at[pl.ds(pl.multiple_of(peer * part, 8), part)],
        lambda sender: shot_slots.at[sender],
        0,
    )
    shot_slots[shot] = grads[pl.ds(pl.multiple_of(shot * part, 8), part)]
    finish(handle)

    def add(slots):
        running = slots[0]
        for index in range(1, slots.shape[0]):
            running = running + slots[index]
        return running

    base = sizes["shot"]
    ready[0] = add(shot_slots)
    handle = stage("net", lambda peer: ready.at[0], lambda sender: net_slots.at[sender], base)
    net_slots[lax.axis_index("net")] = ready[0]
    finish(handle)
    base += sizes["net"]
    ready[1] = add(net_slots)
    handle = stage("band", lambda peer: ready.at[1], lambda sender: band_slots.at[sender], base)
    band_slots[lax.axis_index("band")] = ready[1]
    finish(handle)
    base += sizes["band"]
    ready[2] = add(band_slots)
    handle = stage(
        "shot",
        lambda peer: ready.at[2],
        lambda sender: out.at[pl.ds(pl.multiple_of(sender * part, 8), part)],
        base,
    )
    out[pl.ds(pl.multiple_of(shot * part, 8), part)] = ready[2]
    finish(handle)


def total_grads(grads):
    sizes = {axis: lax.axis_size(axis) for axis in ("shot", "net", "band")}
    part = (grads.shape[0] // sizes["shot"], grads.shape[1])
    f32 = jnp.float32
    count = 2 * sizes["shot"] + sizes["net"] + sizes["band"]
    return pl.pallas_call(
        functools.partial(total_kernel, sizes),
        name="total_grads",
        out_shape=jax.ShapeDtypeStruct(grads.shape, f32),
        in_specs=vmem(1),
        out_specs=vmem(1)[0],
        scratch_shapes=[
            pltpu.VMEM((sizes["shot"],) + part, f32),
            pltpu.VMEM((sizes["net"],) + part, f32),
            pltpu.VMEM((sizes["band"],) + part, f32),
            pltpu.VMEM((3,) + part, f32),
            pltpu.SemaphoreType.DMA((count,)),
            pltpu.SemaphoreType.DMA((count,)),
        ],
        compiler_params=pltpu.CompilerParams(collective_id=2, has_side_effects=True),
    )(grads)


lead = 16


def advance(now, prior, speed):
    middle = now(0)
    wide = jnp.concatenate([middle, jnp.zeros((middle.shape[0], 128), jnp.float32)], 1)
    breadth = middle.shape[1]
    running = 2.0 * coefficients[0] * middle
    for reach in range(1, 5):
        lateral = pltpu.roll(wide, reach, 1) + pltpu.roll(wide, breadth + 128 - reach, 1)
        running = running + coefficients[reach] * (
            now(-reach) + now(reach) + lateral[:, :breadth]
        )
    return 2.0 * middle - prior + speed * running


def wave_kernel(
    bands, near_bands,
    velocity, wave_now, wave_before, adjoint_last, adjoint_after, drive, marked, recorded,
    image,
    states, speeds, near_speed, bursts, injected,
    send, receive, speed_send, speed_receive, near_send, near_receive, burst_send, burst_receive,
):
    shots, rows, breadth = wave_now.shape
    steps = drive.shape[0]
    pairs = steps // 2
    band = lax.axis_index("band")
    tall = rows + 2 * lead
    margin = 8
    upper = pl.ds(lead - 8, 8)
    lower = pl.ds(lead + rows, 8)
    own = pl.ds(lead, rows)
    low_near = lax.min(lax.max(near_bands - band, 0), 1)

    @pl.when(band == 0)
    def _():
        for field in range(2):
            for shot in range(shots):
                states[field, 0, shot, upper] = jnp.zeros((8, breadth), jnp.float32)
                for slot in range(1, steps + 2, 2):
                    states[field, slot, shot, upper] = jnp.zeros((8, breadth), jnp.float32)
        speeds[upper] = jnp.zeros((8, breadth), jnp.float32)

    @pl.when(band == bands - 1)
    def _():
        for field in range(2):
            for shot in range(shots):
                states[field, 0, shot, lower] = jnp.zeros((8, breadth), jnp.float32)
                for slot in range(1, steps + 2, 2):
                    states[field, slot, shot, lower] = jnp.zeros((8, breadth), jnp.float32)
        speeds[lower] = jnp.zeros((8, breadth), jnp.float32)

    barrier = pltpu.get_barrier_semaphore()

    def meet(offset):
        pl.semaphore_signal(
            barrier, inc=1, device_id={"band": band + offset}, device_id_type=MESH
        )

    pl.when(band > 0)(lambda: meet(-1))
    pl.when(band < bands - 1)(lambda: meet(1))
    count = lax.min(band, 1) + lax.min(bands - 1 - band, 1)
    for offset in range(2, near_bands):
        pl.when(band + offset < near_bands)(lambda: meet(offset))
        pl.when((band < near_bands) & (band >= offset))(lambda: meet(-offset))
        count = count + lax.min(lax.max(near_bands - offset - band, 0), 1)
        count = count + low_near * lax.min(lax.max(band - offset + 1, 0), 1)
    pl.semaphore_wait(barrier, count)

    def sides(source_up, source_down, target_up, target_down, sends, receives):
        up = lambda: remote(
            source_up, target_down, sends.at[0], receives.at[0], {"band": band - 1}
        )
        down = lambda: remote(
            source_down, target_up, sends.at[1], receives.at[1], {"band": band + 1}
        )

        def start():
            pl.when(band > 0)(lambda: up().start())
            pl.when(band < bands - 1)(lambda: down().start())

        def finish():
            pl.when(band > 0)(lambda: down().wait_recv())
            pl.when(band < bands - 1)(lambda: up().wait_recv())
            pl.when(band > 0)(lambda: up().wait_send())
            pl.when(band < bands - 1)(lambda: down().wait_send())

        return start, finish

    def input_sides(source, field, slot, place):
        return sides(
            source.at[:, pl.ds(0, 8)],
            source.at[:, pl.ds(rows - 8, 8)],
            states.at[field, slot, :, upper],
            states.at[field, slot, :, lower],
            send.at[field, place],
            receive.at[field, place],
        )

    def state_sides(field, pair):
        slot = 2 * pair + 1
        return sides(
            states.at[field, slot, :, pl.ds(lead, 8)],
            states.at[field, slot, :, pl.ds(lead + rows - 8, 8)],
            states.at[field, slot, :, upper],
            states.at[field, slot, :, lower],
            send.at[field, pair],
            receive.at[field, pair],
        )

    opening = [
        input_sides(wave_now, 0, 1, 0),
        input_sides(wave_before, 0, 0, pairs),
        sides(
            velocity.at[pl.ds(0, 8)],
            velocity.at[pl.ds(rows - 8, 8)],
            speeds.at[upper],
            speeds.at[lower],
            speed_send,
            speed_receive,
        ),
        input_sides(adjoint_last, 1, 1, 0),
        input_sides(adjoint_after, 1, 0, pairs),
    ]
    for start, finish in opening:
        start()

    def near_copy(sender, target, peer):
        return remote(
            velocity,
            near_speed.at[pl.ds(margin + sender * rows, rows)],
            near_send.at[target],
            near_receive.at[sender],
            {"band": peer},
        )

    def each_near(action):
        for sender in range(near_bands):
            for target in range(near_bands):
                if sender != target:
                    action(sender, target)

    each_near(lambda sender, target: pl.when(band == sender)(lambda: near_copy(sender, target, target).start()))

    states[0, 1, :, own] = wave_now[...]
    states[0, 0, :, own] = wave_before[...]
    states[1, 1, :, own] = adjoint_last[...]
    states[1, 0, :, own] = adjoint_after[...]
    for start, finish in opening:
        finish()
    speeds[own] = velocity[...]
    speeds[lead - 8 : lead + rows + 8] = (speeds[lead - 8 : lead + rows + 8] * speed_factor) ** 2

    def grow(field, slot, first, last):
        for shot in range(shots):
            for row in range(first, last, 8):
                states[field, slot + 1, shot, row : row + 8] = advance(
                    lambda reach: states[field, slot, shot, row + reach : row + reach + 8],
                    states[field, slot - 1, shot, row : row + 8],
                    speeds[row : row + 8],
                )
            if field == 0:
                spot = slice(lead + source_depth, lead + source_depth + 1)
                states[0, slot + 1, shot, spot] = (
                    states[0, slot + 1, shot, spot] + drive[slot - 1, shot : shot + 1]
                )

    def pair_step(pair, carry):
        for field in range(2):
            pl.when(pair > 0)(lambda: state_sides(field, pair)[1]())
            grow(field, 2 * pair + 1, lead - 8, lead + rows + 8)
            grow(field, 2 * pair + 2, lead, lead + rows)
            pl.when(pair < pairs - 1)(lambda: state_sides(field, pair + 1)[0]())
        return carry

    lax.fori_loop(0, pairs, pair_step, 0)

    @pl.when(band == 0)
    def _():
        spot = lead + receiver_depth
        for step in range(steps):
            for shot in range(shots):
                injected[step, shot : shot + 1] = (
                    states[0, step + 2, shot, spot : spot + 1] * marked[shot : shot + 1]
                    - recorded[step, shot : shot + 1]
                )

    def burst_copy(target, peer):
        return remote(
            injected, injected, burst_send.at[target], burst_receive, {"band": peer}
        )

    for target in range(1, near_bands):
        pl.when(band == 0)(lambda: burst_copy(target, target).start())
    each_near(
        lambda sender, target: pl.when(band == target)(
            lambda: near_copy(sender, target, sender).wait_recv()
        )
    )
    each_near(
        lambda sender, target: pl.when(band == sender)(
            lambda: near_copy(sender, target, target).wait_send()
        )
    )

    @pl.when(band < near_bands)
    def _():
        start = pl.multiple_of(margin + band * rows, 8)
        near_speed[pl.ds(start, rows)] = velocity[...]
        near_speed[...] = (near_speed[...] * speed_factor) ** 2
        bursts[...] = jnp.zeros(bursts.shape, jnp.float32)

    for target in range(1, near_bands):
        pl.when(band == target)(lambda: burst_copy(target, 0).wait_recv())
        pl.when(band == 0)(lambda: burst_copy(target, target).wait_send())

    @pl.when(band < near_bands)
    def _():
        def burst_step(index, carry):
            now = index % 2
            other = 1 - now
            reached = (index + 2) // 2
            needed = ((band + 1) * rows + 4 * (steps - 1 - index) + 7) // 8
            blocks = lax.min(lax.min(reached, needed), near_bands * rows // 8)

            def block(number, inner):
                row = pl.multiple_of(margin + number * 8, 8)
                for shot in range(shots):
                    tile = bursts[now, shot, pl.ds(row - 8, 24)]
                    bursts[other, shot, pl.ds(row, 8)] = advance(
                        lambda reach: tile[8 + reach : 16 + reach],
                        bursts[other, shot, pl.ds(row, 8)],
                        near_speed[pl.ds(row, 8)],
                        )
                return inner

            lax.fori_loop(0, blocks, block, 0)
            spot = slice(margin + receiver_depth, margin + receiver_depth + 1)
            start = pl.multiple_of(margin + band * rows, 8)
            for shot in range(shots):
                bursts[other, shot, spot] = (
                    bursts[other, shot, spot] + injected[steps - 1 - index, shot : shot + 1]
                )
                states[1, index + 2, shot, own] = (
                    states[1, index + 2, shot, own] + bursts[other, shot, pl.ds(start, rows)]
                )
            return carry

        lax.fori_loop(0, steps, burst_step, 0)

    for row in range(0, rows, 8):
        def accumulate(index, running):
            for shot in range(shots):
                running = running + (
                    states[0, steps + 1 - index, shot, lead + row : lead + row + 8]
                    * states[1, index + 2, shot, lead + row : lead + row + 8]
                )
            return running

        image[row : row + 8] = lax.fori_loop(
            0, steps, accumulate, jnp.zeros((8, breadth), jnp.float32)
        )


def wave_image(
    velocity, wave_now, wave_before, adjoint_last, adjoint_after, drive, marked, recorded
):
    shots, rows, breadth = wave_now.shape
    steps = drive.shape[0]
    bands = lax.axis_size("band")
    reach = receiver_depth + 1 + 4 * (steps - 1)
    near_bands = min(bands, -(-reach // rows))
    f32 = jnp.float32
    dma = pltpu.SemaphoreType.DMA
    tall = rows + 2 * lead
    return pl.pallas_call(
        functools.partial(wave_kernel, bands, near_bands),
        name="wave_image",
        out_shape=jax.ShapeDtypeStruct((rows, breadth), f32),
        in_specs=vmem(8),
        out_specs=vmem(1)[0],
        scratch_shapes=[
            pltpu.VMEM((2, steps + 2, shots, tall, breadth), f32),
            pltpu.VMEM((tall, breadth), f32),
            pltpu.VMEM((near_bands * rows + 16, breadth), f32),
            pltpu.VMEM((2, shots, near_bands * rows + 16, breadth), f32),
            pltpu.VMEM((steps, shots, breadth), f32),
            dma((2, steps // 2 + 1, 2)),
            dma((2, steps // 2 + 1, 2)),
            dma((2,)),
            dma((2,)),
            dma((near_bands,)),
            dma((near_bands,)),
            dma((near_bands,)),
            dma,
        ],
        compiler_params=pltpu.CompilerParams(
            collective_id=3, has_side_effects=True, vmem_limit_bytes=48 * 1024 * 1024
        ),
    )(velocity, wave_now, wave_before, adjoint_last, adjoint_after, drive, marked, recorded)


def halves(values):
    high = values.astype(jnp.bfloat16)
    return high, (values - high.astype(jnp.float32)).astype(jnp.bfloat16)


def dot3(left, right_high, right_low, dims):
    high, low = halves(left)
    height = left.shape[0]
    both = lax.dot_general(
        jnp.concatenate([high, low], 0), right_high, (dims, ((), ())),
        preferred_element_type=jnp.float32,
    )
    rest = lax.dot_general(
        high, right_low, (dims, ((), ())), preferred_element_type=jnp.float32
    )
    return both[:height] + both[height:] + rest


def network_kernel(
    width, first, middle, middle_back, last, layers,
    new_velocity, grads,
    patch_zero, patch_high, patch_low, before_one, hidden, slope_two, last_taps,
):
    length = layers.shape[1]
    channels = middle.shape[0]
    shifts = [down * width + across for down in (-1, 0, 1) for across in (-1, 0, 1)]
    pieces = length // chunk
    flat = ((1,), (0,))
    over = ((1,), (1,))

    for tap, shift in enumerate(shifts):
        patch_zero[tap * 8 : tap * 8 + 8] = pltpu.roll(layers[...], (-shift) % length, 1)

    def spread(source):
        for group in range(channels // 16):
            rows = source[group * 16 : group * 16 + 16]
            for tap, shift in enumerate(shifts):
                high, low = halves(pltpu.roll(rows, (-shift) % length, 1))
                start = tap * channels + group * 16
                patch_high[start : start + 16] = high
                patch_low[start : start + 16] = low

    def each(body, init=0):
        def step(index, carry):
            return body(pl.ds(pl.multiple_of(index * chunk, chunk), chunk), carry)

        return lax.fori_loop(0, pieces, step, init)

    def slope(values):
        squashed = 1.0 / (1.0 + jnp.exp(-values))
        return squashed * (1.0 + values * (1.0 - squashed))

    def silu(values):
        return values / (1.0 + jnp.exp(-values))

    def open_layer(at, carry):
        high, low = halves(patch_zero[:, at])
        both = dot3(first[...], high, low, flat)
        inside = layers[4:5, at] > 0.5
        before = both[:channels]
        before_one[:, at] = before
        hidden[:, at] = jnp.where(inside, silu(before), 0.0)
        slope_two[:, at] = both[channels:]
        return carry

    each(open_layer)
    spread(hidden)

    def middle_layer(at, carry):
        high = patch_high[:, at]
        low = patch_low[:, at]
        before = dot3(middle[...], high, low, flat)
        inside = layers[4:5, at] > 0.5
        owned = layers[5:6, at] > 0.5
        after = jnp.where(inside, silu(before), 0.0)
        hidden[:, at] = after
        fall = jnp.where(inside, slope_two[:, at] * slope(before), 0.0)
        slope_two[:, at] = fall
        after_high, after_low = halves(after)
        last_taps[:, at] = dot3(last[...], after_high, after_low, flat)
        return carry + dot3(jnp.where(owned, fall, 0.0), high, low, over)

    grad_middle = each(middle_layer, jnp.zeros((channels, 9 * channels), jnp.float32))
    spread(slope_two)
    update = layers[0:1]
    for tap, shift in enumerate(shifts):
        update = update + pltpu.roll(last_taps[...], (-shift) % length, 1)[tap : tap + 1]
    new_velocity[...] = update

    def first_grads(at, carry):
        back = dot3(middle_back[...], patch_high[:, at], patch_low[:, at], flat)
        owned = layers[5:6, at] > 0.5
        fall = jnp.where(owned, back * slope(before_one[:, at]), 0.0)
        high, low = halves(patch_zero[:, at])
        return carry + dot3(jnp.concatenate([fall, hidden[:, at]], 0), high, low, over)

    outer = each(first_grads, jnp.zeros((2 * channels, 72), jnp.float32))
    grads[...] = jnp.zeros(grads.shape, jnp.float32)
    grads[:, 0 : 9 * channels] = grad_middle
    start = -(-9 * channels // 128) * 128
    grads[:, start : start + 72] = outer[:channels]
    grads[:, start + 128 : start + 200] = outer[channels:]


def network(layers, width, conv_in, conv_mid, conv_out):
    length = layers.shape[1]
    channels = conv_mid.shape[0]
    f32 = jnp.float32
    taken = conv_in.reshape(channels, 9, 2)
    first = jnp.concatenate(
        [
            jnp.pad(taken, ((0, 0), (0, 0), (0, 6))).reshape(channels, 72),
            jnp.pad(flipped(conv_out)[:, :, None], ((0, 0), (0, 0), (2, 5))).reshape(channels, 72),
        ],
        0,
    )
    last = jnp.pad(conv_out.reshape(9, channels), ((0, 7), (0, 0)))
    start = -(-9 * channels // 128) * 128
    return pl.pallas_call(
        functools.partial(network_kernel, width),
        name="network",
        out_shape=[
            jax.ShapeDtypeStruct((1, length), f32),
            jax.ShapeDtypeStruct((channels, start + 256), f32),
        ],
        in_specs=vmem(5),
        out_specs=vmem(2),
        scratch_shapes=[
            pltpu.VMEM((72, length), f32),
            pltpu.VMEM((9 * channels, length), jnp.bfloat16),
            pltpu.VMEM((9 * channels, length), jnp.bfloat16),
            pltpu.VMEM((channels, length), f32),
            pltpu.VMEM((channels, length), f32),
            pltpu.VMEM((channels, length), f32),
            pltpu.VMEM((16, length), f32),
        ],
        compiler_params=pltpu.CompilerParams(vmem_limit_bytes=48 * 1024 * 1024),
    )(first, conv_mid, flipped(conv_mid), last, layers)


def update_model(imaging, velocity, cotangent, num_steps, shot_count, conv_in, conv_mid, conv_out):
    rows, breadth = velocity.shape
    piece = cotangent.shape[1]
    channels = conv_mid.shape[0]
    bands = lax.axis_size("band")
    groups = lax.axis_size(group_axes)
    image, cot, low, high = gather_pieces(imaging, velocity, cotangent)
    scaled = image[5:-5, piece - 3 : 2 * piece + 3] / float(num_steps * shot_count) ** 0.5
    cot = cot[5:-5, piece - 3 : 2 * piece + 3]
    tall = jnp.concatenate([low[5:], velocity, high[:3]], 0)
    start_col = lax.axis_index(group_axes) * piece
    around = lax.dynamic_slice_in_dim(
        jnp.pad(tall, ((0, 0), (piece, piece))), start_col, 3 * piece, 1
    )[:, piece - 3 : 2 * piece + 3]
    height, width = around.shape
    row_ids = lax.axis_index("band") * rows - 3 + jnp.arange(height)
    col_ids = start_col - 3 + jnp.arange(width)
    inside = ((row_ids >= 0) & (row_ids < rows * bands))[:, None] & (
        (col_ids >= 0) & (col_ids < piece * groups)
    )[None, :]
    owned = np.zeros((height, width), np.float32)
    owned[3:-3, 3:-3] = 1.0
    blank = jnp.zeros((height, width), jnp.float32)
    layers = jnp.stack(
        [around, scaled, cot, cot * owned, inside.astype(jnp.float32), jnp.asarray(owned), blank, blank]
    ).reshape(8, height * width)
    length = -(-height * width // chunk) * chunk
    layers = jnp.pad(layers, ((0, 0), (0, length - height * width)))
    fresh, grads = network(layers, width, conv_in, conv_mid, conv_out)
    new_velocity = fresh[0, : height * width].reshape(height, width)[3:-3, 3:-3]
    grads = total_grads(grads)
    start = -(-9 * channels // 128) * 128
    grad_in = grads[:, start : start + 72].reshape(channels, 9, 8)[:, :, :2].reshape(channels, 18)
    spare = grads[:, start + 128 : start + 200].reshape(channels, 9, 8)[:, ::-1, 3]
    return new_velocity, grad_in, grads[:, : 9 * channels], spare.T.reshape(1, 9 * channels)


def on_device(
    velocity,
    wave_now,
    wave_before,
    adjoint_last,
    adjoint_after,
    wavelet,
    source_col,
    rec_first,
    rec_last,
    rec_count,
    observed,
    conv_in,
    conv_mid,
    conv_out,
    cotangent,
):
    breadth = velocity.shape[1]
    shot_here = wave_now.shape[0]
    num_steps = wavelet.shape[1]
    slots = observed.shape[2]
    columns = jnp.arange(breadth, dtype=jnp.int32)
    source_cols = (columns[None, :] == source_col[:, None]).astype(jnp.float32)
    topmost = (lax.axis_index("band") == 0).astype(jnp.float32)
    drive = wavelet.T[:, :, None] * (source_cols * topmost)[None]
    table = receiver_table(rec_first, rec_last, rec_count, breadth, slots)
    marked = jnp.sum(table, axis=2)
    recorded = jnp.einsum("stk,swk->tsw", observed, table, precision=highest)
    imaging = wave_image(
        velocity, wave_now, wave_before, adjoint_last, adjoint_after, drive, marked, recorded
    )
    group_count = shot_here * lax.axis_size(("shot", "net"))
    return update_model(
        imaging, velocity, cotangent, num_steps, group_count, conv_in, conv_mid, conv_out
    )


def solution(mesh):
    in_specs = (
        P("band", None),
        P(("shot", "net"), "band", None),
        P(("shot", "net"), "band", None),
        P(("shot", "net"), "band", None),
        P(("shot", "net"), "band", None),
        P(("shot", "net"), None),
        P(("shot", "net")),
        P(("shot", "net")),
        P(("shot", "net")),
        P(("shot", "net")),
        P(("shot", "net"), None, None),
        P(),
        P(),
        P(),
        P("band", ("shot", "net")),
    )
    out_specs = (P("band", ("shot", "net")), P(), P(), P())
    return jax.shard_map(
        on_device, mesh=mesh, in_specs=in_specs, out_specs=out_specs, check_vma=False
    )
```

```python
import functools

import jax
import jax.numpy as jnp
import numpy as np
from jax import lax
from jax.experimental import pallas as pl
from jax.experimental.pallas import tpu as pltpu
from jax.sharding import PartitionSpec as P

coefficients = (-205.0 / 72.0, 8.0 / 5.0, -1.0 / 5.0, 8.0 / 315.0, -1.0 / 560.0)
speed_factor = 0.11
source_depth = 2
receiver_depth = 3
highest = lax.Precision.HIGHEST


def receiver_table(rec_first, rec_last, rec_count, breadth, slots):
    columns = jnp.arange(breadth, dtype=jnp.int32)
    slot_ids = jnp.arange(slots, dtype=jnp.int32)
    placed = (
        rec_first[:, None]
        + slot_ids[None, :] * (rec_last - rec_first)[:, None] // (rec_count - 1)[:, None]
    )
    active = slot_ids[None, :] < rec_count[:, None]
    return ((columns[None, :, None] == placed[:, None, :]) & active[:, None, :]).astype(jnp.float32)


def flipped(weights):
    outputs = weights.shape[0]
    channels = weights.shape[1] // 9
    return (
        weights.reshape(outputs, 9, channels)[:, ::-1, :]
        .transpose(2, 1, 0)
        .reshape(channels, 9 * outputs)
    )


MESH = pl.DeviceIdType.MESH
group_axes = ("shot", "net")
chunk = 512


def vmem(count):
    return [pl.BlockSpec(memory_space=pltpu.VMEM)] * count


def remote(source, target, send, receive, device):
    return pltpu.make_async_remote_copy(
        src_ref=source,
        dst_ref=target,
        send_sem=send,
        recv_sem=receive,
        device_id=device,
        device_id_type=MESH,
    )


def gather_kernel(
    groups, nets, bands, image, velocity, cotangent,
    out_image, out_cot, out_low, out_high,
    packed, slots, total, halo, speed_halo,
    send, receive, side_send, side_receive, row_send, row_receive,
):
    rows, breadth = image.shape
    piece = cotangent.shape[1]
    shot = lax.axis_index("shot")
    net = lax.axis_index("net")
    band = lax.axis_index("band")
    me = shot * nets + net

    def member(index):
        return {"shot": index // nets, "net": lax.rem(index, nets)}

    total[1] = jnp.zeros((rows, 3 * piece), jnp.float32)
    halo[...] = jnp.zeros(halo.shape, jnp.float32)
    speed_halo[...] = jnp.zeros(speed_halo.shape, jnp.float32)
    barrier = pltpu.get_barrier_semaphore()
    for step in range(1, groups):
        pl.semaphore_signal(
            barrier, inc=1, device_id=member(lax.rem(me + step, groups)), device_id_type=MESH
        )

    @pl.when(band > 0)
    def _():
        pl.semaphore_signal(barrier, inc=1, device_id={"band": band - 1}, device_id_type=MESH)

    @pl.when(band < bands - 1)
    def _():
        pl.semaphore_signal(barrier, inc=1, device_id={"band": band + 1}, device_id_type=MESH)

    left_half = lax.broadcasted_iota(jnp.int32, (rows, piece), 1) < piece // 2
    blank = jnp.zeros((rows, piece), jnp.float32)
    for index in range(groups):
        first = index * piece
        before = image[:, first - piece : first] if index > 0 else blank
        after = image[:, first + piece : first + 2 * piece] if index < groups - 1 else blank
        packed[index, :, :piece] = image[:, first : first + piece]
        packed[index, :, piece:] = jnp.where(left_half, after, before)
    pl.semaphore_wait(
        barrier, groups - 1 + lax.min(band, 1) + lax.min(bands - 1 - band, 1)
    )

    def scatter(step):
        target = lax.rem(me + step, groups)
        return remote(
            packed.at[target],
            slots.at[step],
            send.at[step],
            receive.at[step],
            member(target),
        )

    for step in range(1, groups):
        scatter(step).start()

    def to_right():
        return remote(
            cotangent, total.at[1, :, pl.ds(0, piece)], side_send.at[0], side_receive.at[0],
            member(me + 1),
        )

    def to_left():
        return remote(
            cotangent, total.at[1, :, pl.ds(2 * piece, piece)], side_send.at[1],
            side_receive.at[1], member(me - 1),
        )

    def speed_up():
        return remote(
            velocity.at[pl.ds(0, 8)], speed_halo.at[1], row_send.at[0], row_receive.at[0],
            {"band": band - 1},
        )

    def speed_down():
        return remote(
            velocity.at[pl.ds(rows - 8, 8)], speed_halo.at[0], row_send.at[1], row_receive.at[1],
            {"band": band + 1},
        )

    def field_up():
        return remote(
            total.at[:, pl.ds(0, 8)], halo.at[1], row_send.at[2], row_receive.at[2],
            {"band": band - 1},
        )

    def field_down():
        return remote(
            total.at[:, pl.ds(rows - 8, 8)], halo.at[0], row_send.at[3], row_receive.at[3],
            {"band": band + 1},
        )

    pl.when(me < groups - 1)(lambda: to_right().start())
    pl.when(me > 0)(lambda: to_left().start())
    pl.when(band > 0)(lambda: speed_up().start())
    pl.when(band < bands - 1)(lambda: speed_down().start())

    slots[0] = packed[me]
    for step in range(1, groups):
        scatter(step).wait_recv()
    summed = slots[0]
    for step in range(1, groups):
        summed = summed + slots[step]
    total[0, :, :piece] = summed[:, piece:]
    total[0, :, piece : 2 * piece] = summed[:, :piece]
    total[0, :, 2 * piece :] = summed[:, piece:]
    pl.when(me > 0)(lambda: to_right().wait_recv())
    pl.when(me < groups - 1)(lambda: to_left().wait_recv())
    total[1, :, piece : 2 * piece] = cotangent[...]
    pl.when(band > 0)(lambda: field_up().start())
    pl.when(band < bands - 1)(lambda: field_down().start())
    for step in range(1, groups):
        scatter(step).wait_send()
    pl.when(me < groups - 1)(lambda: to_right().wait_send())
    pl.when(me > 0)(lambda: to_left().wait_send())
    pl.when(band > 0)(lambda: speed_up().wait_send())
    pl.when(band < bands - 1)(lambda: speed_down().wait_send())
    pl.when(band > 0)(lambda: speed_down().wait_recv())
    pl.when(band < bands - 1)(lambda: speed_up().wait_recv())
    pl.when(band > 0)(lambda: field_up().wait_send())
    pl.when(band < bands - 1)(lambda: field_down().wait_send())
    pl.when(band > 0)(lambda: field_down().wait_recv())
    pl.when(band < bands - 1)(lambda: field_up().wait_recv())
    for which, target in ((0, out_image), (1, out_cot)):
        target[0:8] = halo[0, which]
        target[8 : 8 + rows] = total[which]
        target[8 + rows :] = halo[1, which]
    out_low[...] = speed_halo[0]
    out_high[...] = speed_halo[1]


def gather_pieces(image, velocity, cotangent):
    rows, breadth = image.shape
    piece = cotangent.shape[1]
    groups = lax.axis_size(group_axes)
    nets = lax.axis_size("net")
    bands = lax.axis_size("band")
    f32 = jnp.float32
    dma = pltpu.SemaphoreType.DMA
    return pl.pallas_call(
        functools.partial(gather_kernel, groups, nets, bands),
        name="gather_pieces",
        out_shape=[jax.ShapeDtypeStruct((rows + 16, 3 * piece), f32)] * 2
        + [jax.ShapeDtypeStruct((8, breadth), f32)] * 2,
        in_specs=vmem(3),
        out_specs=vmem(4),
        scratch_shapes=[
            pltpu.VMEM((groups, rows, 2 * piece), f32),
            pltpu.VMEM((groups, rows, 2 * piece), f32),
            pltpu.VMEM((2, rows, 3 * piece), f32),
            pltpu.VMEM((2, 2, 8, 3 * piece), f32),
            pltpu.VMEM((2, 8, breadth), f32),
            dma((groups,)),
            dma((groups,)),
            dma((2,)),
            dma((2,)),
            dma((4,)),
            dma((4,)),
        ],
        compiler_params=pltpu.CompilerParams(collective_id=1, has_side_effects=True),
    )(image, velocity, cotangent)


def total_kernel(sizes, grads, out, shot_slots, net_slots, band_slots, ready, send, receive):
    part = grads.shape[0] // sizes["shot"]
    barrier = pltpu.get_barrier_semaphore()
    count = 0
    for axis, size in sizes.items():
        me = lax.axis_index(axis)
        for step in range(1, size):
            pl.semaphore_signal(
                barrier, inc=1, device_id={axis: lax.rem(me + step, size)}, device_id_type=MESH
            )
            count += 1
    pl.semaphore_wait(barrier, count)
    base = 0

    def stage(axis, source, target_of, base):
        size = sizes[axis]
        me = lax.axis_index(axis)

        def copy(step, sender):
            peer = lax.rem(me + step, size)
            return remote(
                source(peer), target_of(sender), send.at[base + step], receive.at[base + sender],
                {axis: peer},
            )

        for step in range(1, size):
            copy(step, me).start()
        return copy, size, me

    def finish(handle):
        copy, size, me = handle
        for step in range(1, size):
            copy(step, lax.rem(me + step, size)).wait_recv()
        for step in range(1, size):
            copy(step, me).wait_send()

    shot = lax.axis_index("shot")
    handle = stage(
        "shot",
        lambda peer: grads.at[pl.ds(pl.multiple_of(peer * part, 8), part)],
        lambda sender: shot_slots.at[sender],
        0,
    )
    shot_slots[shot] = grads[pl.ds(pl.multiple_of(shot * part, 8), part)]
    finish(handle)

    def add(slots):
        running = slots[0]
        for index in range(1, slots.shape[0]):
            running = running + slots[index]
        return running

    base = sizes["shot"]
    ready[0] = add(shot_slots)
    handle = stage("net", lambda peer: ready.at[0], lambda sender: net_slots.at[sender], base)
    net_slots[lax.axis_index("net")] = ready[0]
    finish(handle)
    base += sizes["net"]
    ready[1] = add(net_slots)
    handle = stage("band", lambda peer: ready.at[1], lambda sender: band_slots.at[sender], base)
    band_slots[lax.axis_index("band")] = ready[1]
    finish(handle)
    base += sizes["band"]
    ready[2] = add(band_slots)
    handle = stage(
        "shot",
        lambda peer: ready.at[2],
        lambda sender: out.at[pl.ds(pl.multiple_of(sender * part, 8), part)],
        base,
    )
    out[pl.ds(pl.multiple_of(shot * part, 8), part)] = ready[2]
    finish(handle)


def total_grads(grads):
    sizes = {axis: lax.axis_size(axis) for axis in ("shot", "net", "band")}
    part = (grads.shape[0] // sizes["shot"], grads.shape[1])
    f32 = jnp.float32
    count = 2 * sizes["shot"] + sizes["net"] + sizes["band"]
    return pl.pallas_call(
        functools.partial(total_kernel, sizes),
        name="total_grads",
        out_shape=jax.ShapeDtypeStruct(grads.shape, f32),
        in_specs=vmem(1),
        out_specs=vmem(1)[0],
        scratch_shapes=[
            pltpu.VMEM((sizes["shot"],) + part, f32),
            pltpu.VMEM((sizes["net"],) + part, f32),
            pltpu.VMEM((sizes["band"],) + part, f32),
            pltpu.VMEM((3,) + part, f32),
            pltpu.SemaphoreType.DMA((count,)),
            pltpu.SemaphoreType.DMA((count,)),
        ],
        compiler_params=pltpu.CompilerParams(collective_id=2, has_side_effects=True),
    )(grads)


lead = 16


def advance(now, prior, speed):
    middle = now(0)
    wide = jnp.concatenate([middle, jnp.zeros((middle.shape[0], 128), jnp.float32)], 1)
    breadth = middle.shape[1]
    running = 2.0 * coefficients[0] * middle
    for reach in range(1, 5):
        lateral = pltpu.roll(wide, reach, 1) + pltpu.roll(wide, breadth + 128 - reach, 1)
        running = running + coefficients[reach] * (
            now(-reach) + now(reach) + lateral[:, :breadth]
        )
    return 2.0 * middle - prior + speed * running


def wave_kernel(
    bands, near_bands,
    velocity, wave_now, wave_before, adjoint_last, adjoint_after, drive, marked, recorded,
    image,
    states, speeds, near_speed, bursts, injected,
    send, receive, speed_send, speed_receive, near_send, near_receive, burst_send, burst_receive,
):
    shots, rows, breadth = wave_now.shape
    steps = drive.shape[0]
    pairs = steps // 2
    band = lax.axis_index("band")
    tall = rows + 2 * lead
    margin = 8
    upper = pl.ds(lead - 8, 8)
    lower = pl.ds(lead + rows, 8)
    own = pl.ds(lead, rows)
    low_near = lax.min(lax.max(near_bands - band, 0), 1)

    @pl.when(band == 0)
    def _():
        for field in range(2):
            for shot in range(shots):
                states[field, 0, shot, upper] = jnp.zeros((8, breadth), jnp.float32)
                for slot in range(1, steps + 2, 2):
                    states[field, slot, shot, upper] = jnp.zeros((8, breadth), jnp.float32)
        speeds[upper] = jnp.zeros((8, breadth), jnp.float32)

    @pl.when(band == bands - 1)
    def _():
        for field in range(2):
            for shot in range(shots):
                states[field, 0, shot, lower] = jnp.zeros((8, breadth), jnp.float32)
                for slot in range(1, steps + 2, 2):
                    states[field, slot, shot, lower] = jnp.zeros((8, breadth), jnp.float32)
        speeds[lower] = jnp.zeros((8, breadth), jnp.float32)

    barrier = pltpu.get_barrier_semaphore()

    def meet(offset):
        pl.semaphore_signal(
            barrier, inc=1, device_id={"band": band + offset}, device_id_type=MESH
        )

    pl.when(band > 0)(lambda: meet(-1))
    pl.when(band < bands - 1)(lambda: meet(1))
    count = lax.min(band, 1) + lax.min(bands - 1 - band, 1)
    for offset in range(2, near_bands):
        pl.when(band + offset < near_bands)(lambda: meet(offset))
        pl.when((band < near_bands) & (band >= offset))(lambda: meet(-offset))
        count = count + lax.min(lax.max(near_bands - offset - band, 0), 1)
        count = count + low_near * lax.min(lax.max(band - offset + 1, 0), 1)
    pl.semaphore_wait(barrier, count)

    def sides(source_up, source_down, target_up, target_down, sends, receives):
        up = lambda: remote(
            source_up, target_down, sends.at[0], receives.at[0], {"band": band - 1}
        )
        down = lambda: remote(
            source_down, target_up, sends.at[1], receives.at[1], {"band": band + 1}
        )

        def start():
            pl.when(band > 0)(lambda: up().start())
            pl.when(band < bands - 1)(lambda: down().start())

        def finish():
            pl.when(band > 0)(lambda: down().wait_recv())
            pl.when(band < bands - 1)(lambda: up().wait_recv())
            pl.when(band > 0)(lambda: up().wait_send())
            pl.when(band < bands - 1)(lambda: down().wait_send())

        return start, finish

    def input_sides(source, field, slot, place):
        return sides(
            source.at[:, pl.ds(0, 8)],
            source.at[:, pl.ds(rows - 8, 8)],
            states.at[field, slot, :, upper],
            states.at[field, slot, :, lower],
            send.at[field, place],
            receive.at[field, place],
        )

    def state_sides(field, pair):
        slot = 2 * pair + 1
        return sides(
            states.at[field, slot, :, pl.ds(lead, 8)],
            states.at[field, slot, :, pl.ds(lead + rows - 8, 8)],
            states.at[field, slot, :, upper],
            states.at[field, slot, :, lower],
            send.at[field, pair],
            receive.at[field, pair],
        )

    opening = [
        input_sides(wave_now, 0, 1, 0),
        input_sides(wave_before, 0, 0, pairs),
        sides(
            velocity.at[pl.ds(0, 8)],
            velocity.at[pl.ds(rows - 8, 8)],
            speeds.at[upper],
            speeds.at[lower],
            speed_send,
            speed_receive,
        ),
        input_sides(adjoint_last, 1, 1, 0),
        input_sides(adjoint_after, 1, 0, pairs),
    ]
    for start, finish in opening:
        start()

    def near_copy(sender, target, peer):
        return remote(
            velocity,
            near_speed.at[pl.ds(margin + sender * rows, rows)],
            near_send.at[target],
            near_receive.at[sender],
            {"band": peer},
        )

    def each_near(action):
        for sender in range(near_bands):
            for target in range(near_bands):
                if sender != target:
                    action(sender, target)

    each_near(lambda sender, target: pl.when(band == sender)(lambda: near_copy(sender, target, target).start()))

    states[0, 1, :, own] = wave_now[...]
    states[0, 0, :, own] = wave_before[...]
    states[1, 1, :, own] = adjoint_last[...]
    states[1, 0, :, own] = adjoint_after[...]
    for start, finish in opening:
        finish()
    speeds[own] = velocity[...]
    speeds[lead - 8 : lead + rows + 8] = (speeds[lead - 8 : lead + rows + 8] * speed_factor) ** 2

    inner = list(range(lead + 8, lead + rows - 8, 8))
    edges = [row for row in range(lead, lead + rows, 8) if row not in inner]
    outer = [lead - 8] + edges + [lead + rows]

    def grow(field, slot, chosen):
        for shot in range(shots):
            for row in chosen:
                states[field, slot + 1, shot, row : row + 8] = advance(
                    lambda reach: states[field, slot, shot, row + reach : row + reach + 8],
                    states[field, slot - 1, shot, row : row + 8],
                    speeds[row : row + 8],
                )
            if field == 0 and lead in chosen:
                spot = slice(lead + source_depth, lead + source_depth + 1)
                states[0, slot + 1, shot, spot] = (
                    states[0, slot + 1, shot, spot] + drive[slot - 1, shot : shot + 1]
                )

    def pair_step(pair, carry):
        for field in range(2):
            grow(field, 2 * pair + 1, inner)
            pl.when(pair > 0)(lambda: state_sides(field, pair)[1]())
            grow(field, 2 * pair + 1, outer)
            grow(field, 2 * pair + 2, edges)
            pl.when(pair < pairs - 1)(lambda: state_sides(field, pair + 1)[0]())
            grow(field, 2 * pair + 2, inner)
        return carry

    lax.fori_loop(0, pairs, pair_step, 0)

    @pl.when(band == 0)
    def _():
        spot = lead + receiver_depth
        for step in range(steps):
            for shot in range(shots):
                injected[step, shot : shot + 1] = (
                    states[0, step + 2, shot, spot : spot + 1] * marked[shot : shot + 1]
                    - recorded[step, shot : shot + 1]
                )

    def burst_copy(target, peer):
        return remote(
            injected, injected, burst_send.at[target], burst_receive, {"band": peer}
        )

    for target in range(1, near_bands):
        pl.when(band == 0)(lambda: burst_copy(target, target).start())
    each_near(
        lambda sender, target: pl.when(band == target)(
            lambda: near_copy(sender, target, sender).wait_recv()
        )
    )
    each_near(
        lambda sender, target: pl.when(band == sender)(
            lambda: near_copy(sender, target, target).wait_send()
        )
    )

    @pl.when(band < near_bands)
    def _():
        start = pl.multiple_of(margin + band * rows, 8)
        near_speed[pl.ds(start, rows)] = velocity[...]
        near_speed[...] = (near_speed[...] * speed_factor) ** 2
        bursts[...] = jnp.zeros(bursts.shape, jnp.float32)

    for target in range(1, near_bands):
        pl.when(band == target)(lambda: burst_copy(target, 0).wait_recv())
        pl.when(band == 0)(lambda: burst_copy(target, target).wait_send())

    @pl.when(band < near_bands)
    def _():
        def burst_step(index, carry):
            now = index % 2
            other = 1 - now
            reached = (index + 2) // 2
            needed = ((band + 1) * rows + 4 * (steps - 1 - index) + 7) // 8
            blocks = lax.min(lax.min(reached, needed), near_bands * rows // 8)

            def block(number, inner):
                row = pl.multiple_of(margin + number * 8, 8)
                for shot in range(shots):
                    tile = bursts[now, shot, pl.ds(row - 8, 24)]
                    bursts[other, shot, pl.ds(row, 8)] = advance(
                        lambda reach: tile[8 + reach : 16 + reach],
                        bursts[other, shot, pl.ds(row, 8)],
                        near_speed[pl.ds(row, 8)],
                        )
                return inner

            lax.fori_loop(0, blocks, block, 0)
            spot = slice(margin + receiver_depth, margin + receiver_depth + 1)
            start = pl.multiple_of(margin + band * rows, 8)
            for shot in range(shots):
                bursts[other, shot, spot] = (
                    bursts[other, shot, spot] + injected[steps - 1 - index, shot : shot + 1]
                )
                states[1, index + 2, shot, own] = (
                    states[1, index + 2, shot, own] + bursts[other, shot, pl.ds(start, rows)]
                )
            return carry

        lax.fori_loop(0, steps, burst_step, 0)

    for row in range(0, rows, 8):
        def accumulate(index, running):
            for shot in range(shots):
                running = running + (
                    states[0, steps + 1 - index, shot, lead + row : lead + row + 8]
                    * states[1, index + 2, shot, lead + row : lead + row + 8]
                )
            return running

        image[row : row + 8] = lax.fori_loop(
            0, steps, accumulate, jnp.zeros((8, breadth), jnp.float32)
        )


def wave_image(
    velocity, wave_now, wave_before, adjoint_last, adjoint_after, drive, marked, recorded
):
    shots, rows, breadth = wave_now.shape
    steps = drive.shape[0]
    bands = lax.axis_size("band")
    reach = receiver_depth + 1 + 4 * (steps - 1)
    near_bands = min(bands, -(-reach // rows))
    f32 = jnp.float32
    dma = pltpu.SemaphoreType.DMA
    tall = rows + 2 * lead
    return pl.pallas_call(
        functools.partial(wave_kernel, bands, near_bands),
        name="wave_image",
        out_shape=jax.ShapeDtypeStruct((rows, breadth), f32),
        in_specs=vmem(8),
        out_specs=vmem(1)[0],
        scratch_shapes=[
            pltpu.VMEM((2, steps + 2, shots, tall, breadth), f32),
            pltpu.VMEM((tall, breadth), f32),
            pltpu.VMEM((near_bands * rows + 16, breadth), f32),
            pltpu.VMEM((2, shots, near_bands * rows + 16, breadth), f32),
            pltpu.VMEM((steps, shots, breadth), f32),
            dma((2, steps // 2 + 1, 2)),
            dma((2, steps // 2 + 1, 2)),
            dma((2,)),
            dma((2,)),
            dma((near_bands,)),
            dma((near_bands,)),
            dma((near_bands,)),
            dma,
        ],
        compiler_params=pltpu.CompilerParams(
            collective_id=3, has_side_effects=True, vmem_limit_bytes=48 * 1024 * 1024
        ),
    )(velocity, wave_now, wave_before, adjoint_last, adjoint_after, drive, marked, recorded)


def halves(values):
    high = values.astype(jnp.bfloat16)
    return high, (values - high.astype(jnp.float32)).astype(jnp.bfloat16)


def dot3(left, right_high, right_low, dims):
    high, low = halves(left)
    height = left.shape[0]
    both = lax.dot_general(
        jnp.concatenate([high, low], 0), right_high, (dims, ((), ())),
        preferred_element_type=jnp.float32,
    )
    rest = lax.dot_general(
        high, right_low, (dims, ((), ())), preferred_element_type=jnp.float32
    )
    return both[:height] + both[height:] + rest


def network_kernel(
    width, first, middle, middle_back, last, layers,
    new_velocity, grads,
    patch_zero, patch_high, patch_low, before_one, hidden, slope_two, last_taps,
):
    length = layers.shape[1]
    channels = middle.shape[0]
    shifts = [down * width + across for down in (-1, 0, 1) for across in (-1, 0, 1)]
    pieces = length // chunk
    flat = ((1,), (0,))
    over = ((1,), (1,))

    for tap, shift in enumerate(shifts):
        patch_zero[tap * 8 : tap * 8 + 8] = pltpu.roll(layers[...], (-shift) % length, 1)

    def spread(source):
        for group in range(channels // 16):
            rows = source[group * 16 : group * 16 + 16]
            for tap, shift in enumerate(shifts):
                high, low = halves(pltpu.roll(rows, (-shift) % length, 1))
                start = tap * channels + group * 16
                patch_high[start : start + 16] = high
                patch_low[start : start + 16] = low

    def each(body, init=0):
        def step(index, carry):
            return body(pl.ds(pl.multiple_of(index * chunk, chunk), chunk), carry)

        return lax.fori_loop(0, pieces, step, init)

    def slope(values):
        squashed = 1.0 / (1.0 + jnp.exp(-values))
        return squashed * (1.0 + values * (1.0 - squashed))

    def silu(values):
        return values / (1.0 + jnp.exp(-values))

    def open_layer(at, carry):
        high, low = halves(patch_zero[:, at])
        both = dot3(first[...], high, low, flat)
        inside = layers[4:5, at] > 0.5
        before = both[:channels]
        before_one[:, at] = before
        hidden[:, at] = jnp.where(inside, silu(before), 0.0)
        slope_two[:, at] = both[channels:]
        return carry

    each(open_layer)
    spread(hidden)

    def middle_layer(at, carry):
        high = patch_high[:, at]
        low = patch_low[:, at]
        before = dot3(middle[...], high, low, flat)
        inside = layers[4:5, at] > 0.5
        owned = layers[5:6, at] > 0.5
        after = jnp.where(inside, silu(before), 0.0)
        hidden[:, at] = after
        fall = jnp.where(inside, slope_two[:, at] * slope(before), 0.0)
        slope_two[:, at] = fall
        after_high, after_low = halves(after)
        last_taps[:, at] = dot3(last[...], after_high, after_low, flat)
        return carry + dot3(jnp.where(owned, fall, 0.0), high, low, over)

    grad_middle = each(middle_layer, jnp.zeros((channels, 9 * channels), jnp.float32))
    spread(slope_two)
    update = layers[0:1]
    for tap, shift in enumerate(shifts):
        update = update + pltpu.roll(last_taps[...], (-shift) % length, 1)[tap : tap + 1]
    new_velocity[...] = update

    def first_grads(at, carry):
        back = dot3(middle_back[...], patch_high[:, at], patch_low[:, at], flat)
        owned = layers[5:6, at] > 0.5
        fall = jnp.where(owned, back * slope(before_one[:, at]), 0.0)
        high, low = halves(patch_zero[:, at])
        return carry + dot3(jnp.concatenate([fall, hidden[:, at]], 0), high, low, over)

    outer = each(first_grads, jnp.zeros((2 * channels, 72), jnp.float32))
    grads[...] = jnp.zeros(grads.shape, jnp.float32)
    grads[:, 0 : 9 * channels] = grad_middle
    start = -(-9 * channels // 128) * 128
    grads[:, start : start + 72] = outer[:channels]
    grads[:, start + 128 : start + 200] = outer[channels:]


def network(layers, width, conv_in, conv_mid, conv_out):
    length = layers.shape[1]
    channels = conv_mid.shape[0]
    f32 = jnp.float32
    taken = conv_in.reshape(channels, 9, 2)
    first = jnp.concatenate(
        [
            jnp.pad(taken, ((0, 0), (0, 0), (0, 6))).reshape(channels, 72),
            jnp.pad(flipped(conv_out)[:, :, None], ((0, 0), (0, 0), (2, 5))).reshape(channels, 72),
        ],
        0,
    )
    last = jnp.pad(conv_out.reshape(9, channels), ((0, 7), (0, 0)))
    start = -(-9 * channels // 128) * 128
    return pl.pallas_call(
        functools.partial(network_kernel, width),
        name="network",
        out_shape=[
            jax.ShapeDtypeStruct((1, length), f32),
            jax.ShapeDtypeStruct((channels, start + 256), f32),
        ],
        in_specs=vmem(5),
        out_specs=vmem(2),
        scratch_shapes=[
            pltpu.VMEM((72, length), f32),
            pltpu.VMEM((9 * channels, length), jnp.bfloat16),
            pltpu.VMEM((9 * channels, length), jnp.bfloat16),
            pltpu.VMEM((channels, length), f32),
            pltpu.VMEM((channels, length), f32),
            pltpu.VMEM((channels, length), f32),
            pltpu.VMEM((16, length), f32),
        ],
        compiler_params=pltpu.CompilerParams(vmem_limit_bytes=48 * 1024 * 1024),
    )(first, conv_mid, flipped(conv_mid), last, layers)


def update_model(imaging, velocity, cotangent, num_steps, shot_count, conv_in, conv_mid, conv_out):
    rows, breadth = velocity.shape
    piece = cotangent.shape[1]
    channels = conv_mid.shape[0]
    bands = lax.axis_size("band")
    groups = lax.axis_size(group_axes)
    image, cot, low, high = gather_pieces(imaging, velocity, cotangent)
    scaled = image[5:-5, piece - 3 : 2 * piece + 3] / float(num_steps * shot_count) ** 0.5
    cot = cot[5:-5, piece - 3 : 2 * piece + 3]
    tall = jnp.concatenate([low[5:], velocity, high[:3]], 0)
    start_col = lax.axis_index(group_axes) * piece
    around = lax.dynamic_slice_in_dim(
        jnp.pad(tall, ((0, 0), (piece, piece))), start_col, 3 * piece, 1
    )[:, piece - 3 : 2 * piece + 3]
    height, width = around.shape
    row_ids = lax.axis_index("band") * rows - 3 + jnp.arange(height)
    col_ids = start_col - 3 + jnp.arange(width)
    inside = ((row_ids >= 0) & (row_ids < rows * bands))[:, None] & (
        (col_ids >= 0) & (col_ids < piece * groups)
    )[None, :]
    owned = np.zeros((height, width), np.float32)
    owned[3:-3, 3:-3] = 1.0
    blank = jnp.zeros((height, width), jnp.float32)
    layers = jnp.stack(
        [around, scaled, cot, cot * owned, inside.astype(jnp.float32), jnp.asarray(owned), blank, blank]
    ).reshape(8, height * width)
    length = -(-height * width // chunk) * chunk
    layers = jnp.pad(layers, ((0, 0), (0, length - height * width)))
    fresh, grads = network(layers, width, conv_in, conv_mid, conv_out)
    new_velocity = fresh[0, : height * width].reshape(height, width)[3:-3, 3:-3]
    grads = total_grads(grads)
    start = -(-9 * channels // 128) * 128
    grad_in = grads[:, start : start + 72].reshape(channels, 9, 8)[:, :, :2].reshape(channels, 18)
    spare = grads[:, start + 128 : start + 200].reshape(channels, 9, 8)[:, ::-1, 3]
    return new_velocity, grad_in, grads[:, : 9 * channels], spare.T.reshape(1, 9 * channels)


def on_device(
    velocity,
    wave_now,
    wave_before,
    adjoint_last,
    adjoint_after,
    wavelet,
    source_col,
    rec_first,
    rec_last,
    rec_count,
    observed,
    conv_in,
    conv_mid,
    conv_out,
    cotangent,
):
    breadth = velocity.shape[1]
    shot_here = wave_now.shape[0]
    num_steps = wavelet.shape[1]
    slots = observed.shape[2]
    columns = jnp.arange(breadth, dtype=jnp.int32)
    source_cols = (columns[None, :] == source_col[:, None]).astype(jnp.float32)
    topmost = (lax.axis_index("band") == 0).astype(jnp.float32)
    drive = wavelet.T[:, :, None] * (source_cols * topmost)[None]
    table = receiver_table(rec_first, rec_last, rec_count, breadth, slots)
    marked = jnp.sum(table, axis=2)
    recorded = jnp.einsum("stk,swk->tsw", observed, table, precision=highest)
    imaging = wave_image(
        velocity, wave_now, wave_before, adjoint_last, adjoint_after, drive, marked, recorded
    )
    group_count = shot_here * lax.axis_size(("shot", "net"))
    return update_model(
        imaging, velocity, cotangent, num_steps, group_count, conv_in, conv_mid, conv_out
    )


def solution(mesh):
    in_specs = (
        P("band", None),
        P(("shot", "net"), "band", None),
        P(("shot", "net"), "band", None),
        P(("shot", "net"), "band", None),
        P(("shot", "net"), "band", None),
        P(("shot", "net"), None),
        P(("shot", "net")),
        P(("shot", "net")),
        P(("shot", "net")),
        P(("shot", "net")),
        P(("shot", "net"), None, None),
        P(),
        P(),
        P(),
        P("band", ("shot", "net")),
    )
    out_specs = (P("band", ("shot", "net")), P(), P(), P())
    return jax.shard_map(
        on_device, mesh=mesh, in_specs=in_specs, out_specs=out_specs, check_vma=False
    )
```
